32 devices in a mesh: dp: 8 (over z, y), fsdp: 4 (over x, core).
Axes of the slice: x: 2, y: 2, z: 4, core: 2. Of those that a mesh axis runs over, the one named last changes fastest.
Arguments:
- tokens: bfloat16 [4096, 896], P(('dp', 'fsdp')), may hold values from -6 to 6
- cotangent: bfloat16 [4096, 896], P(('dp', 'fsdp')), may hold values from -6 to 6
- segments: int32 [32, 128], P(('dp', 'fsdp')), may hold values from 0 to 7, never falling along the last dimension, each value on 1 to 64 neighbouring positions
- gain_att: float32 [896], replicated, may hold values from 0.5 to 1.5
- gain_ffn: float32 [896], replicated, may hold values from 0.5 to 1.5
- qkv_bias: float32 [1152], replicated, may hold values from -3 to 3
- w_attention: bfloat16 [2048, 896], P(('dp', 'fsdp')), may hold values from -0.31 to 0.31
- w_gate: bfloat16 [4864, 896], P(('dp', 'fsdp')), may hold values from -0.1875 to 0.1875
- w_up: bfloat16 [4864, 896], P(('dp', 'fsdp')), may hold values from -0.1875 to 0.1875
- w_down: bfloat16 [4864, 896], P(('dp', 'fsdp')), may hold values from -0.078125 to 0.078125
Outputs:
- layer_out: bfloat16 [4096, 896], P(('dp', 'fsdp'))
- grad_tokens: bfloat16 [4096, 896], P(('dp', 'fsdp'))
- grad_gainatt: float32 [896], replicated
- grad_gainffn: float32 [896], replicated
- grad_bias: float32 [1152], replicated
- grad_attention: float32 [2048, 896], P(('dp', 'fsdp'))
- grad_gate: float32 [4864, 896], P(('dp', 'fsdp'))
- grad_up: float32 [4864, 896], P(('dp', 'fsdp'))
- grad_down: float32 [4864, 896], P(('dp', 'fsdp'))
The draws below stay inside these ranges and needn't reach their ends.
Inputs may be any that keep to these rules, and one draw needn't show every extreme that they name: `segments`: in each device's row of 128 tokens the numbers never fall; each device holds exactly 8 sequences, each of 1 to 64 tokens.
All inputs are finite; a program needn't handle non-finite values.
Results may differ from the reference program's by a relative error of at most 0.012.
The reference program's roundings to bfloat16 on the way count: a program that leaves them out, or rounds other values in their place, can miss the bound.
Values may be sent and summed in bfloat16 or wider, within the bound.
A program may use at most 320 MiB of HBM per device.

```python
import math
import jax
import jax.numpy as jnp
import numpy as np
from jax import lax

D = 896
HEADS = 14
KV_HEADS = 2
HEAD_DIM = 64
FF = 4864
ROWS = 128
SEQS = 8
MOST = 64
QKV = 1152
ATT = 2048
TOKENS = 4096
N_DP = 8
N_FSDP = 4


def draw_tokens(key, part):
    entry_key = jax.random.fold_in(key, 11)
    column_key = jax.random.fold_in(key, 12)
    row_key = jax.random.fold_in(key, 13)
    entries = jnp.clip(jax.random.normal(entry_key, (TOKENS, D), jnp.float32), -4.0, 4.0)
    lower_log = jnp.log(jnp.float32(0.3))
    upper_log = jnp.log(jnp.float32(3.0))
    column = jnp.exp(jax.random.uniform(column_key, (1, D), jnp.float32, lower_log, upper_log))
    rowwise = jnp.exp(jax.random.uniform(row_key, (TOKENS, 1), jnp.float32, lower_log, upper_log))
    return jnp.clip(entries * column * rowwise, -6.0, 6.0).astype(jnp.bfloat16)


def draw_w_attention(key, part):
    entry_key = jax.random.fold_in(key, 21)
    entries = jnp.clip(jax.random.normal(entry_key, (ATT, D), jnp.float32), -3.0, 3.0)
    row_index = jnp.arange(ATT, dtype=jnp.int32)[:, None]
    spread = jnp.where(row_index < QKV, jnp.float32(0.034), jnp.float32(0.1))
    return (entries * spread).astype(jnp.bfloat16)


def steps_of(rng, dims, pieces, low, largest):
    level = 1.0
    for axis_at, shards_of in pieces:
        draws = jax.random.uniform(jax.random.fold_in(jax.random.fold_in(rng, 6), axis_at), (shards_of,), jnp.float32, low / len(pieces), largest / len(pieces))
        level = level * jnp.repeat(jnp.exp(draws), dims[axis_at] // shards_of).reshape((-1,) + (1,) * (len(dims) - 1 - axis_at))
    return level


def length_profile(count, total, limit, skew):
    portions = [(1 << 20) // math.isqrt(standing ** skew) + 1 for standing in range(2, count + 1)]
    surplus, given = total - limit - (count - 1), [1] * (count - 1)
    while surplus > 0:
        free = [i for i in range(count - 1) if given[i] < limit]
        whole, left = sum([portions[i] for i in free]), surplus
        for i in free:
            addition = min(limit - given[i], max(1, left * portions[i] // whole), surplus)
            given[i] = given[i] + addition
            surplus = surplus - addition
    return np.array([limit] + given)


def ragged(stream_key, number_of, total, reach, skew):
    if number_of == 2:
        one = jax.random.randint(stream_key, (), max(1, total - reach), min(reach, total - 1) + 1)
        return jnp.stack([one, total - one])
    lengths = jnp.asarray(length_profile(number_of, total, reach, skew), jnp.int32)
    twos = (number_of - 1) // 2
    giver, taker = lengths[1:1 + 2 * twos:2], lengths[2:2 + 2 * twos:2]
    margin = jnp.minimum(giver - 1, reach - taker)
    moved = jax.random.randint(jax.random.fold_in(stream_key, 1), (twos,), 0, 1 << 20) % (margin + 1)
    lengths = lengths.at[1:1 + 2 * twos:2].set(giver - moved).at[2:2 + 2 * twos:2].set(taker + moved)
    return lengths[jax.random.permutation(jax.random.fold_in(stream_key, 2), number_of)]


def centred(own_key, dims, scale, reach, shards=(), kind=jnp.bfloat16):
    values = scale * jax.random.normal(own_key, dims, jnp.float32)
    if shards:
        values = values * steps_of(own_key, dims, shards, -0.22, 0.18)
    return jnp.clip(values, -reach, reach).astype(kind)


def setup_inputs(seed: int = 0) -> dict:
    splits = jax.random.split(jax.random.key(seed), 11)
    tokens = draw_tokens(jax.random.fold_in(splits[10], 71), 0)
    cotangent = centred(splits[1], (TOKENS, D), 1.0, 6.0, ((0, 32),))
    segments = jax.vmap(lambda own: jnp.searchsorted(jnp.cumsum(ragged(own, SEQS, ROWS, MOST, 2)), jnp.arange(ROWS), side="right"))(jax.random.split(splits[2], (N_DP * N_FSDP))).reshape((N_DP * N_FSDP, ROWS)).astype(jnp.int32)
    gain_att = jnp.clip(1.0 + 0.1 * jax.random.normal(splits[3], (D,), jnp.float32), 0.5, 1.5)
    gain_ffn = jnp.clip(1.0 + 0.1 * jax.random.normal(splits[4], (D,), jnp.float32), 0.5, 1.5)
    qkv_bias = centred(splits[5], (QKV,), 0.5, 3.0, (), jnp.float32)
    w_attention = draw_w_attention(jax.random.fold_in(splits[10], 71), 0)
    w_gate = centred(splits[7], (FF, D), D ** -0.5, 0.1875, ((0, 32),))
    w_up = centred(splits[8], (FF, D), D ** -0.5, 0.1875, ((0, 32),))
    w_down = centred(splits[9], (FF, D), FF ** -0.5, 0.078125, ((0, 32),))
    return dict(tokens=tokens, cotangent=cotangent, segments=segments, gain_att=gain_att, gain_ffn=gain_ffn, qkv_bias=qkv_bias, w_attention=w_attention, w_gate=w_gate, w_up=w_up, w_down=w_down)


EPS = 1e-06
THETA = 1000000.0

def rotary_tables(segments):
    length = segments.shape[-1]
    before = lax.optimization_barrier(jnp.sum((segments[..., None, :] < segments[..., :, None]).astype(jnp.int32), -1))
    positions = jnp.arange(length, dtype=jnp.int32)[None, :] - before
    halfway = HEAD_DIM // 2
    frequency = THETA ** (-2.0 * jnp.arange(halfway, dtype=jnp.float32) / HEAD_DIM)
    angles = positions.astype(jnp.float32)[..., None] * frequency
    cosine = jnp.concatenate([jnp.cos(angles), jnp.cos(angles)], -1)[:, :, None, :]
    sines = jnp.concatenate([jnp.sin(angles), jnp.sin(angles)], -1)[:, :, None, :]
    return (cosine, sines)

def rotate(tensor):
    halfway = tensor.shape[-1] // 2
    return jnp.concatenate([-tensor[..., halfway:], tensor[..., :halfway]], -1)

def unrotate(tensor):
    halfway = tensor.shape[-1] // 2
    return jnp.concatenate([tensor[..., halfway:], -tensor[..., :halfway]], -1)

def visible(segments):
    length = segments.shape[-1]
    matches = segments[..., :, None] == segments[..., None, :]
    index = jnp.arange(length, dtype=jnp.int32)
    causal = index[None, :] <= index[:, None]
    return matches & causal[None]

def attend_scores(query_bf, key_bf, allowed):
    scores = jnp.einsum('grkpd,gskd->gkprs', query_bf.astype(jnp.float32), key_bf.astype(jnp.float32)) * HEAD_DIM ** (-0.5)
    return jnp.where(allowed[:, None, None], scores, -1e+30)

def norm_back(grad_in, values, scale, gain):
    weighted = grad_in * gain
    return scale * weighted - values * scale ** 3 * lax.optimization_barrier(jnp.mean(weighted * values, -1, keepdims=True))

def plain_dot(left, right):
    return jnp.dot(left, right, preferred_element_type=jnp.float32)

def group_pass(token_block, segment_block, cot_block, gain_att, gain_ffn, qkv_bias, w_attention, w_gate, w_up, w_down):
    groups, rows_here = segment_block.shape
    flat_rows = groups * rows_here
    q_width = HEADS * HEAD_DIM
    kv_width = KV_HEADS * HEAD_DIM
    repeat_count = HEADS // KV_HEADS
    w_qkv = w_attention[:QKV]
    w_out = w_attention[QKV:]
    resid_in = token_block.reshape(flat_rows, D).astype(jnp.float32)
    scale_att = lax.rsqrt(lax.optimization_barrier(jnp.mean(resid_in * resid_in, -1, keepdims=True)) + EPS)
    normed_att = (resid_in * scale_att * gain_att).astype(jnp.bfloat16)
    projected = plain_dot(normed_att, w_qkv.T) + qkv_bias
    cosine, sines = rotary_tables(segment_block)
    queries = projected[:, :q_width].reshape(groups, rows_here, HEADS, HEAD_DIM)
    keys_raw = projected[:, q_width:q_width + kv_width].reshape(groups, rows_here, KV_HEADS, HEAD_DIM)
    values_raw = projected[:, q_width + kv_width:].reshape(groups, rows_here, KV_HEADS, HEAD_DIM)
    query_bf = (queries * cosine + rotate(queries) * sines).astype(jnp.bfloat16).reshape(groups, rows_here, KV_HEADS, repeat_count, HEAD_DIM)
    key_bf = (keys_raw * cosine + rotate(keys_raw) * sines).astype(jnp.bfloat16)
    value_bf = values_raw.astype(jnp.bfloat16)
    allowed = visible(segment_block)
    scores = attend_scores(query_bf, key_bf, allowed)
    log_total = jnp.log(lax.optimization_barrier(jnp.sum(jnp.exp(scores), -1, keepdims=True)))
    soft_bf = jnp.exp(scores - log_total).astype(jnp.bfloat16)
    attended = jnp.einsum('gkprs,gskd->grkpd', soft_bf.astype(jnp.float32), value_bf.astype(jnp.float32))
    attended = attended.reshape(flat_rows, q_width).astype(jnp.bfloat16)
    middle = resid_in + plain_dot(attended, w_out)
    scale_ffn = lax.rsqrt(lax.optimization_barrier(jnp.mean(middle * middle, -1, keepdims=True)) + EPS)
    normed_ffn = (middle * scale_ffn * gain_ffn).astype(jnp.bfloat16)
    gate_pre = plain_dot(normed_ffn, w_gate.T)
    up_pre = plain_dot(normed_ffn, w_up.T)
    sigmoid_gate = jax.nn.sigmoid(gate_pre)
    hidden_act = (gate_pre * sigmoid_gate * up_pre).astype(jnp.bfloat16)
    layer_out = (middle + plain_dot(hidden_act, w_down)).astype(jnp.bfloat16)
    grad_out = cot_block.reshape(flat_rows, D)
    grad_hidden = plain_dot(grad_out, w_down.T)
    gate_back = (grad_hidden * up_pre * sigmoid_gate * (1.0 + gate_pre * (1.0 - sigmoid_gate))).astype(jnp.bfloat16)
    up_back = (grad_hidden * gate_pre * sigmoid_gate).astype(jnp.bfloat16)
    grad_normed = plain_dot(gate_back, w_gate) + plain_dot(up_back, w_up)
    grad_middle = grad_out.astype(jnp.float32) + norm_back(grad_normed, middle, scale_ffn, gain_ffn)
    middle_bf = grad_middle.astype(jnp.bfloat16)
    grad_attended = plain_dot(middle_bf, w_out.T).astype(jnp.bfloat16)
    grad_attended = grad_attended.reshape(groups, rows_here, KV_HEADS, repeat_count, HEAD_DIM)
    scores_again = attend_scores(query_bf, key_bf, allowed)
    soft = jnp.exp(scores_again - log_total)
    grad_soft = jnp.einsum('grkpd,gskd->gkprs', grad_attended.astype(jnp.float32), value_bf.astype(jnp.float32))
    grad_scores = (soft * (grad_soft - lax.optimization_barrier(jnp.sum(soft * grad_soft, -1, keepdims=True))) * HEAD_DIM ** (-0.5)).astype(jnp.bfloat16)
    grad_queries = jnp.einsum('gkprs,gskd->grkpd', grad_scores.astype(jnp.float32), key_bf.astype(jnp.float32))
    grad_queries = grad_queries.reshape(groups, rows_here, HEADS, HEAD_DIM)
    grad_keys = jnp.einsum('gkprs,grkpd->gskd', grad_scores.astype(jnp.float32), query_bf.astype(jnp.float32))
    grad_values = jnp.einsum('gkprs,grkpd->gskd', soft.astype(jnp.bfloat16).astype(jnp.float32), grad_attended.astype(jnp.float32))
    grad_queries = grad_queries * cosine + unrotate(grad_queries * sines)
    grad_keys = grad_keys * cosine + unrotate(grad_keys * sines)
    grad_projected = jnp.concatenate([grad_queries.reshape(flat_rows, q_width), grad_keys.reshape(flat_rows, kv_width), grad_values.reshape(flat_rows, kv_width)], -1)
    projected_bf = grad_projected.astype(jnp.bfloat16)
    grad_inputs = plain_dot(projected_bf, w_qkv)
    grad_tokens = (grad_middle + norm_back(grad_inputs, resid_in, scale_att, gain_att)).astype(jnp.bfloat16)
    grad_attention = jnp.concatenate([plain_dot(projected_bf.T, normed_att), plain_dot(attended.T, middle_bf)], 0)
    gradients = (lax.optimization_barrier(jnp.sum(grad_inputs * resid_in * scale_att, 0)), lax.optimization_barrier(jnp.sum(grad_normed * middle * scale_ffn, 0)), lax.optimization_barrier(jnp.sum(grad_projected, 0)), grad_attention, plain_dot(gate_back.T, normed_ffn), plain_dot(up_back.T, normed_ffn), plain_dot(hidden_act.T, grad_out))
    return (layer_out, grad_tokens, gradients)

def reference(tokens, cotangent, segments, gain_att, gain_ffn, qkv_bias, w_attention, w_gate, w_up, w_down):
    devices = N_DP * N_FSDP
    per_block = math.gcd(devices, max(1, 4096 // ROWS))
    blocks_total = devices // per_block
    token_blocks = tokens.reshape(blocks_total, per_block, ROWS, D)
    cot_blocks = cotangent.reshape(blocks_total, per_block, ROWS, D)
    segment_blocks = segments.reshape(blocks_total, per_block, ROWS)
    initial = (jnp.zeros((D,), jnp.float32), jnp.zeros((D,), jnp.float32), jnp.zeros((QKV,), jnp.float32), jnp.zeros((ATT, D), jnp.float32), jnp.zeros((FF, D), jnp.float32), jnp.zeros((FF, D), jnp.float32), jnp.zeros((FF, D), jnp.float32))

    def advance(carry, element):
        token_block, segment_block, cot_block = element
        layer_out, grad_tokens, gradients = group_pass(token_block, segment_block, cot_block, gain_att, gain_ffn, qkv_bias, w_attention, w_gate, w_up, w_down)
        return (tuple((total + extra for total, extra in zip(carry, gradients))), (layer_out, grad_tokens))
    totals, (layer_out, grad_tokens) = lax.scan(advance, initial, (token_blocks, segment_blocks, cot_blocks))
    return (layer_out.reshape(TOKENS, D), grad_tokens.reshape(TOKENS, D), totals[0], totals[1], totals[2], totals[3], totals[4], totals[5], totals[6])
```

```python
import jax
import jax.numpy as jnp
from jax import lax
from jax.sharding import PartitionSpec as P

HEADS = 14
KV_HEADS = 2
HEAD_DIM = 64
QKV = 1152


EPS = 1e-06
THETA = 1000000.0


def rotary_tables(segments):
    length = segments.shape[-1]
    before = jnp.sum((segments[..., None, :] < segments[..., :, None]).astype(jnp.int32), -1)
    positions = jnp.arange(length, dtype=jnp.int32)[None, :] - before
    halfway = HEAD_DIM // 2
    frequency = THETA ** (-2.0 * jnp.arange(halfway, dtype=jnp.float32) / HEAD_DIM)
    angles = positions.astype(jnp.float32)[..., None] * frequency
    cosine = jnp.concatenate([jnp.cos(angles), jnp.cos(angles)], -1)[:, :, None, :]
    sines = jnp.concatenate([jnp.sin(angles), jnp.sin(angles)], -1)[:, :, None, :]
    return (cosine, sines)


def rotate(tensor):
    halfway = tensor.shape[-1] // 2
    return jnp.concatenate([-tensor[..., halfway:], tensor[..., :halfway]], -1)


def unrotate(tensor):
    halfway = tensor.shape[-1] // 2
    return jnp.concatenate([tensor[..., halfway:], -tensor[..., :halfway]], -1)


def visible(segments):
    length = segments.shape[-1]
    matches = segments[..., :, None] == segments[..., None, :]
    index = jnp.arange(length, dtype=jnp.int32)
    causal = index[None, :] <= index[:, None]
    return matches & causal[None]


def attend_scores(query_bf, key_bf, allowed):
    scores = jnp.einsum(
        "grkpd,gskd->gkprs", query_bf, key_bf, preferred_element_type=jnp.float32
    ) * HEAD_DIM ** (-0.5)
    return jnp.where(allowed[:, None, None], scores, -1e30)


def norm_back(grad_in, values, scale, gain):
    weighted = grad_in * gain
    return scale * weighted - values * scale**3 * jnp.mean(weighted * values, -1, keepdims=True)


def plain_dot(left, right):
    return jnp.dot(left, right, preferred_element_type=jnp.float32)


def proj_dot(left, right):
    return lax.dot_general(
        left, right, (((1,), (1,)), ((), ())), preferred_element_type=jnp.float32
    )


def outer_dot(left, right):
    return lax.dot_general(
        left, right, (((0,), (0,)), ((), ())), preferred_element_type=jnp.float32
    )


BOTH = ("dp", "fsdp")


def gather(shard, axes):
    return lax.all_gather(shard, axes, axis=0, tiled=True)


def scatter_sum(terms, axes):
    return lax.psum_scatter(terms, axes, scatter_dimension=0, tiled=True)


def on_device(
    tokens, cotangent, segments, gain_att, gain_ffn, qkv_bias, w_attention, w_gate, w_up, w_down
):
    w_all = gather(w_attention, BOTH)
    w_qkv, w_out = w_all[:QKV], w_all[QKV:]
    width = tokens.shape[1]
    w_feed = gather(jnp.concatenate([w_gate, w_up, w_down], 1), "fsdp")
    g_gate, g_up, g_down = w_feed[:, :width], w_feed[:, width : 2 * width], w_feed[:, 2 * width :]
    cot_group = gather(cotangent, "dp")
    rows_here = tokens.shape[0]
    q_width = HEADS * HEAD_DIM
    kv_width = KV_HEADS * HEAD_DIM
    repeat_count = HEADS // KV_HEADS
    resid_in = tokens.astype(jnp.float32)
    scale_att = lax.rsqrt(jnp.mean(resid_in * resid_in, -1, keepdims=True) + EPS)
    normed_att = (resid_in * scale_att * gain_att).astype(jnp.bfloat16)
    projected = proj_dot(normed_att, w_qkv) + qkv_bias
    cosine, sines = rotary_tables(segments)
    queries = projected[:, :q_width].reshape(1, rows_here, HEADS, HEAD_DIM)
    keys_raw = projected[:, q_width : q_width + kv_width].reshape(1, rows_here, KV_HEADS, HEAD_DIM)
    values_raw = projected[:, q_width + kv_width :].reshape(1, rows_here, KV_HEADS, HEAD_DIM)
    query_bf = (
        (queries * cosine + rotate(queries) * sines)
        .astype(jnp.bfloat16)
        .reshape(1, rows_here, KV_HEADS, repeat_count, HEAD_DIM)
    )
    key_bf = (keys_raw * cosine + rotate(keys_raw) * sines).astype(jnp.bfloat16)
    value_bf = values_raw.astype(jnp.bfloat16)
    allowed = visible(segments)
    scores = attend_scores(query_bf, key_bf, allowed)
    log_total = jnp.log(jnp.sum(jnp.exp(scores), -1, keepdims=True))
    soft_bf = jnp.exp(scores - log_total).astype(jnp.bfloat16)
    attended = jnp.einsum(
        "gkprs,gskd->grkpd", soft_bf, value_bf, preferred_element_type=jnp.float32
    )
    attended = attended.reshape(rows_here, q_width).astype(jnp.bfloat16)
    middle = resid_in + plain_dot(attended, w_out)
    scale_ffn = lax.rsqrt(jnp.mean(middle * middle, -1, keepdims=True) + EPS)
    normed_ffn = (middle * scale_ffn * gain_ffn).astype(jnp.bfloat16)
    normed_group = gather(normed_ffn, "dp")
    gate_pre = proj_dot(normed_group, g_gate)
    up_pre = proj_dot(normed_group, g_up)
    grad_hidden = proj_dot(cot_group, g_down)
    sigmoid_gate = jax.nn.sigmoid(gate_pre)
    hidden_act = (gate_pre * sigmoid_gate * up_pre).astype(jnp.bfloat16)
    gate_back = (
        grad_hidden * up_pre * sigmoid_gate * (1.0 + gate_pre * (1.0 - sigmoid_gate))
    ).astype(jnp.bfloat16)
    up_back = (grad_hidden * gate_pre * sigmoid_gate).astype(jnp.bfloat16)
    normed_terms = plain_dot(gate_back, g_gate) + plain_dot(up_back, g_up)
    normed_part = scatter_sum(normed_terms.astype(jnp.bfloat16), "dp").astype(jnp.float32)
    down_terms = plain_dot(hidden_act, g_down).astype(jnp.bfloat16)
    down_part = scatter_sum(down_terms, "dp").astype(jnp.float32)
    feed_terms = jnp.concatenate(
        [
            outer_dot(gate_back, normed_group),
            outer_dot(up_back, normed_group),
            outer_dot(hidden_act, cot_group),
        ],
        1,
    ).astype(jnp.bfloat16)
    feed_grads = scatter_sum(feed_terms, "fsdp").astype(jnp.float32)
    layer_out = (middle + down_part).astype(jnp.bfloat16)
    grad_middle = cotangent.astype(jnp.float32) + norm_back(
        normed_part, middle, scale_ffn, gain_ffn
    )
    middle_bf = grad_middle.astype(jnp.bfloat16)
    grad_attended = proj_dot(middle_bf, w_out).astype(jnp.bfloat16)
    grad_attended = grad_attended.reshape(1, rows_here, KV_HEADS, repeat_count, HEAD_DIM)
    scores_again = attend_scores(query_bf, key_bf, allowed)
    soft = jnp.exp(scores_again - log_total)
    grad_soft = jnp.einsum(
        "grkpd,gskd->gkprs", grad_attended, value_bf, preferred_element_type=jnp.float32
    )
    grad_scores = (
        soft * (grad_soft - jnp.sum(soft * grad_soft, -1, keepdims=True)) * HEAD_DIM ** (-0.5)
    ).astype(jnp.bfloat16)
    grad_queries = jnp.einsum(
        "gkprs,gskd->grkpd", grad_scores, key_bf, preferred_element_type=jnp.float32
    )
    grad_queries = grad_queries.reshape(1, rows_here, HEADS, HEAD_DIM)
    grad_keys = jnp.einsum(
        "gkprs,grkpd->gskd", grad_scores, query_bf, preferred_element_type=jnp.float32
    )
    grad_values = jnp.einsum(
        "gkprs,grkpd->gskd",
        soft.astype(jnp.bfloat16),
        grad_attended,
        preferred_element_type=jnp.float32,
    )
    grad_queries = grad_queries * cosine + unrotate(grad_queries * sines)
    grad_keys = grad_keys * cosine + unrotate(grad_keys * sines)
    grad_projected = jnp.concatenate(
        [
            grad_queries.reshape(rows_here, q_width),
            grad_keys.reshape(rows_here, kv_width),
            grad_values.reshape(rows_here, kv_width),
        ],
        -1,
    )
    projected_bf = grad_projected.astype(jnp.bfloat16)
    grad_inputs = plain_dot(projected_bf, w_qkv)
    grad_tokens = (grad_middle + norm_back(grad_inputs, resid_in, scale_att, gain_att)).astype(
        jnp.bfloat16
    )
    attention_term = jnp.concatenate(
        [outer_dot(projected_bf, normed_att), outer_dot(attended, middle_bf)], 0
    )
    grad_attention = scatter_sum(attention_term.astype(jnp.bfloat16), BOTH).astype(jnp.float32)
    small_terms = jnp.concatenate(
        [
            jnp.sum(grad_inputs * resid_in * scale_att, 0),
            jnp.sum(normed_part * middle * scale_ffn, 0),
            jnp.sum(grad_projected, 0),
        ]
    )
    small_sums = jnp.sum(gather(small_terms[None], BOTH), 0)
    return (
        layer_out,
        grad_tokens,
        small_sums[:width],
        small_sums[width : 2 * width],
        small_sums[2 * width :],
        grad_attention,
        feed_grads[:, :width],
        feed_grads[:, width : 2 * width],
        feed_grads[:, 2 * width :],
    )


def solution(mesh):
    placed = (
        P(("dp", "fsdp"), None),
        P(("dp", "fsdp"), None),
        P(("dp", "fsdp"), None),
        P(),
        P(),
        P(),
        P(("dp", "fsdp"), None),
        P(("dp", "fsdp"), None),
        P(("dp", "fsdp"), None),
        P(("dp", "fsdp"), None),
    )
    return jax.shard_map(
        on_device,
        mesh=mesh,
        in_specs=placed,
        out_specs=(
            P(("dp", "fsdp"), None),
            P(("dp", "fsdp"), None),
            P(),
            P(),
            P(),
            P(("dp", "fsdp"), None),
            P(("dp", "fsdp"), None),
            P(("dp", "fsdp"), None),
            P(("dp", "fsdp"), None),
        ),
        check_vma=False,
    )
```

```python
import jax
import jax.numpy as jnp
import functools
from jax import lax
from jax.experimental import pallas as pl
from jax.experimental.pallas import tpu as pltpu
from jax.sharding import Mesh, PartitionSpec as P

HEADS = 14
KV_HEADS = 2
HEAD_DIM = 64
QKV = 1152


EPS = 1e-06
THETA = 1000000.0


def rotary_tables(segments):
    length = segments.shape[-1]
    before = jnp.sum((segments[..., None, :] < segments[..., :, None]).astype(jnp.int32), -1)
    positions = jnp.arange(length, dtype=jnp.int32)[None, :] - before
    halfway = HEAD_DIM // 2
    frequency = THETA ** (-2.0 * jnp.arange(halfway, dtype=jnp.float32) / HEAD_DIM)
    angles = positions.astype(jnp.float32)[..., None] * frequency
    cosine = jnp.concatenate([jnp.cos(angles), jnp.cos(angles)], -1)[:, :, None, :]
    sines = jnp.concatenate([jnp.sin(angles), jnp.sin(angles)], -1)[:, :, None, :]
    return (cosine, sines)


def rotate(tensor):
    halfway = tensor.shape[-1] // 2
    return jnp.concatenate([-tensor[..., halfway:], tensor[..., :halfway]], -1)


def unrotate(tensor):
    halfway = tensor.shape[-1] // 2
    return jnp.concatenate([tensor[..., halfway:], -tensor[..., :halfway]], -1)


def visible(segments):
    length = segments.shape[-1]
    matches = segments[..., :, None] == segments[..., None, :]
    index = jnp.arange(length, dtype=jnp.int32)
    causal = index[None, :] <= index[:, None]
    return matches & causal[None]


def attend_scores(query_bf, key_bf, allowed):
    scores = jnp.einsum(
        "grkpd,gskd->gkprs", query_bf, key_bf, preferred_element_type=jnp.float32
    ) * HEAD_DIM ** (-0.5)
    return jnp.where(allowed[:, None, None], scores, -1e30)


def norm_back(grad_in, values, scale, gain):
    weighted = grad_in * gain
    return scale * weighted - values * scale**3 * jnp.mean(weighted * values, -1, keepdims=True)


def plain_dot(left, right):
    return jnp.dot(left, right, preferred_element_type=jnp.float32)


def proj_dot(left, right):
    return lax.dot_general(
        left, right, (((1,), (1,)), ((), ())), preferred_element_type=jnp.float32
    )


def outer_dot(left, right):
    return lax.dot_general(
        left, right, (((0,), (0,)), ((), ())), preferred_element_type=jnp.float32
    )


PLANE = ("y", "x", "c")
BOTH = ("z",) + PLANE
OTHERS = ((1, 1), (0, 1), (1, 0))
MESH_ID = pl.DeviceIdType.MESH


def gather(shard, axes):
    return lax.all_gather(shard, axes, axis=0, tiled=True)


def scatter_sum(terms, axes):
    return lax.psum_scatter(terms, axes, scatter_dimension=0, tiled=True)


def here():
    return tuple(lax.axis_index(name) for name in BOTH)


def at_device(z, y, x, c):
    return {"z": z, "y": y, "x": x, "c": c}


def greet(count):
    z, y, x, c = here()
    barrier = pltpu.get_barrier_semaphore()
    targets = [at_device(lax.rem(z + k, count), y, x, c) for k in range(1, count)]
    targets += [at_device(z, y ^ dy, x ^ dx, c) for dy, dx in OTHERS]
    targets.append(at_device(z, y, x, 1 - c))
    for target in targets:
        pl.semaphore_signal(barrier, inc=1, device_id=target, device_id_type=MESH_ID)
    pl.semaphore_wait(barrier, len(targets))


def remote(source, target, send, recv, device):
    return pltpu.make_async_remote_copy(
        src_ref=source,
        dst_ref=target,
        send_sem=send,
        recv_sem=recv,
        device_id=device,
        device_id_type=MESH_ID,
    )


def gather_kernel(count, shard, out, own_sem, z_send, z_recv, p_send, p_recv, c_send, c_recv):
    z, y, x, c = here()
    greet(count)
    slot = z if count > 1 else 0
    own = pltpu.make_async_copy(shard, out.at[slot, y, x, c], own_sem)
    own.start()
    along_z = []
    for k in range(1, count):
        copy = remote(
            shard,
            out.at[slot, y, x, c],
            z_send.at[k - 1],
            z_recv.at[k - 1],
            at_device(lax.rem(z + k, count), y, x, c),
        )
        copy.start()
        along_z.append(copy)
    sent = []
    for k in range(count):
        if k:
            along_z[k - 1].wait_recv()
        held = lax.rem(z - k + count, count) if count > 1 else 0
        block = out.at[held, y, x, c]
        source = block if k else shard
        for j, (dy, dx) in enumerate(OTHERS):
            copy = remote(
                source, block, p_send.at[k, j], p_recv.at[k, j], at_device(z, y ^ dy, x ^ dx, c)
            )
            copy.start()
            sent.append((copy, k, j, held))
        copy = remote(source, block, c_send.at[k, 3], c_recv.at[k, 3], at_device(z, y, x, 1 - c))
        copy.start()
        along_z.append(copy)
    passed = []
    for copy, k, j, held in sent:
        dy, dx = OTHERS[j]
        copy.wait_recv()
        block = out.at[held, y ^ dy, x ^ dx, c]
        onward = remote(block, block, c_send.at[k, j], c_recv.at[k, j], at_device(z, y, x, 1 - c))
        onward.start()
        passed.append(onward)
    for copy, k, j, held in sent:
        copy.wait_send()
    for at, copy in enumerate(along_z):
        copy.wait_send()
        if at >= count - 1:
            copy.wait_recv()
    for copy in passed:
        copy.wait()
    own.wait()


def kernel_gather(shard, count, ident):
    rows, width = shard.shape
    dma = pltpu.SemaphoreType.DMA
    out = pl.pallas_call(
        functools.partial(gather_kernel, count),
        out_shape=jax.ShapeDtypeStruct((count, 2, 2, 2, rows, width), shard.dtype),
        in_specs=[pl.BlockSpec(memory_space=pltpu.VMEM)],
        out_specs=pl.BlockSpec(memory_space=pl.ANY),
        scratch_shapes=[
            dma(()),
            dma((3,)),
            dma((3,)),
            dma((count, 3)),
            dma((count, 3)),
            dma((count, 4)),
            dma((count, 4)),
        ],
        compiler_params=pltpu.CompilerParams(collective_id=ident, has_side_effects=True),
        cost_estimate=pl.CostEstimate(
            flops=20_000_000_000, bytes_accessed=8 * count * rows * width * 2, transcendentals=0
        ),
    )(shard)
    return out.reshape(count * 8 * rows, width)


def scatter_kernel(
    count, terms, out, c_buf, s_buf, p_buf, total, zs_buf, zr_buf,
    c_send, c_recv, p_send, p_recv, z_send, z_recv,
):
    z, y, x, c = here()
    greet(count)
    pieces = OTHERS + ((0, 0),)
    across = []
    for j, (dy, dx) in enumerate(pieces):
        copy = remote(
            terms.at[:, y ^ dy, x ^ dx, 1 - c],
            c_buf.at[j],
            c_send.at[j],
            c_recv.at[j],
            at_device(z, y, x, 1 - c),
        )
        copy.start()
        across.append(copy)
    plane = []
    for j, (dy, dx) in enumerate(pieces):
        across[j].wait_recv()
        for k in range(count):
            pair = terms[k, y ^ dy, x ^ dx, c].astype(jnp.float32) + c_buf[j, k].astype(jnp.float32)
            if j < 3:
                s_buf[j, k] = pair.astype(jnp.bfloat16)
            else:
                total[k] = pair
        if j < 3:
            copy = remote(
                s_buf.at[j],
                p_buf.at[j],
                p_send.at[j],
                p_recv.at[j],
                at_device(z, y ^ dy, x ^ dx, c),
            )
            copy.start()
            plane.append(copy)
    for copy in plane:
        copy.wait_recv()
    if count == 1:
        out[...] = (
            total[0]
            + p_buf[0, 0].astype(jnp.float32)
            + p_buf[1, 0].astype(jnp.float32)
            + p_buf[2, 0].astype(jnp.float32)
        )
    along = []
    for k in range(1, count):
        other = lax.rem(z + k, count)
        zs_buf[k - 1] = (
            total[other]
            + p_buf[0, other].astype(jnp.float32)
            + p_buf[1, other].astype(jnp.float32)
            + p_buf[2, other].astype(jnp.float32)
        ).astype(jnp.bfloat16)
        copy = remote(
            zs_buf.at[k - 1],
            zr_buf.at[k - 1],
            z_send.at[k - 1],
            z_recv.at[k - 1],
            at_device(other, y, x, c),
        )
        copy.start()
        along.append(copy)
    if count > 1:
        kept = (
            total[z]
            + p_buf[0, z].astype(jnp.float32)
            + p_buf[1, z].astype(jnp.float32)
            + p_buf[2, z].astype(jnp.float32)
        )
        for k in range(1, count):
            along[k - 1].wait_recv()
            kept = kept + zr_buf[k - 1].astype(jnp.float32)
        out[...] = kept
    for copy in across + plane + along:
        copy.wait_send()


def kernel_scatter(terms, count, ident):
    rows, width = terms.shape[0] // (8 * count), terms.shape[1]
    dma = pltpu.SemaphoreType.DMA
    block = (rows, width)
    extra = block if count > 1 else (16, 128)
    return pl.pallas_call(
        functools.partial(scatter_kernel, count),
        out_shape=jax.ShapeDtypeStruct(block, jnp.float32),
        in_specs=[pl.BlockSpec(memory_space=pltpu.VMEM)],
        out_specs=pl.BlockSpec(memory_space=pltpu.VMEM),
        scratch_shapes=[
            pltpu.VMEM((4, count) + block, jnp.bfloat16),
            pltpu.VMEM((3, count) + block, jnp.bfloat16),
            pltpu.VMEM((3, count) + block, jnp.bfloat16),
            pltpu.VMEM((count,) + block, jnp.float32),
            pltpu.VMEM((3,) + extra, jnp.bfloat16),
            pltpu.VMEM((3,) + extra, jnp.bfloat16),
            dma((4,)),
            dma((4,)),
            dma((3,)),
            dma((3,)),
            dma((3,)),
            dma((3,)),
        ],
        compiler_params=pltpu.CompilerParams(collective_id=ident, has_side_effects=True),
        cost_estimate=pl.CostEstimate(
            flops=20_000_000_000, bytes_accessed=8 * count * rows * width * 2, transcendentals=0
        ),
    )(terms.reshape((count, 2, 2, 2) + block))


def gather_over(shard, axes, ident, kernels):
    if not kernels:
        return gather(shard, axes)
    return kernel_gather(shard, lax.axis_size("z") if axes == BOTH else 1, ident)


def scatter_over(terms, axes, ident, kernels):
    if not kernels:
        return scatter_sum(terms, axes).astype(jnp.float32)
    return kernel_scatter(terms, lax.axis_size("z") if axes == BOTH else 1, ident)


def on_device(
    kernels, tokens, cotangent, segments, gain_att, gain_ffn, qkv_bias, w_attention, w_gate, w_up, w_down
):
    w_all = gather_over(w_attention, BOTH, 0, kernels)
    w_qkv, w_out = w_all[:QKV], w_all[QKV:]
    width = tokens.shape[1]
    w_feed = gather(jnp.concatenate([w_gate, w_up, w_down], 1), "z")
    g_gate, g_up, g_down = w_feed[:, :width], w_feed[:, width : 2 * width], w_feed[:, 2 * width :]
    rows_here = tokens.shape[0]
    q_width = HEADS * HEAD_DIM
    kv_width = KV_HEADS * HEAD_DIM
    repeat_count = HEADS // KV_HEADS
    resid_in = tokens.astype(jnp.float32)
    scale_att = lax.rsqrt(jnp.mean(resid_in * resid_in, -1, keepdims=True) + EPS)
    normed_att = (resid_in * scale_att * gain_att).astype(jnp.bfloat16)
    projected = proj_dot(normed_att, w_qkv) + qkv_bias
    cosine, sines = rotary_tables(segments)
    queries = projected[:, :q_width].reshape(1, rows_here, HEADS, HEAD_DIM)
    keys_raw = projected[:, q_width : q_width + kv_width].reshape(1, rows_here, KV_HEADS, HEAD_DIM)
    values_raw = projected[:, q_width + kv_width :].reshape(1, rows_here, KV_HEADS, HEAD_DIM)
    query_bf = (
        (queries * cosine + rotate(queries) * sines)
        .astype(jnp.bfloat16)
        .reshape(1, rows_here, KV_HEADS, repeat_count, HEAD_DIM)
    )
    key_bf = (keys_raw * cosine + rotate(keys_raw) * sines).astype(jnp.bfloat16)
    value_bf = values_raw.astype(jnp.bfloat16)
    allowed = visible(segments)
    scores = attend_scores(query_bf, key_bf, allowed)
    log_total = jnp.log(jnp.sum(jnp.exp(scores), -1, keepdims=True))
    soft_bf = jnp.exp(scores - log_total).astype(jnp.bfloat16)
    attended = jnp.einsum(
        "gkprs,gskd->grkpd", soft_bf, value_bf, preferred_element_type=jnp.float32
    )
    attended = attended.reshape(rows_here, q_width).astype(jnp.bfloat16)
    middle = resid_in + plain_dot(attended, w_out)
    scale_ffn = lax.rsqrt(jnp.mean(middle * middle, -1, keepdims=True) + EPS)
    normed_ffn = (middle * scale_ffn * gain_ffn).astype(jnp.bfloat16)
    pair_group = gather_over(jnp.concatenate([normed_ffn, cotangent], 1), PLANE, 1, kernels)
    normed_group, cot_group = pair_group[:, :width], pair_group[:, width:]
    gate_pre = proj_dot(normed_group, g_gate)
    up_pre = proj_dot(normed_group, g_up)
    grad_hidden = proj_dot(cot_group, g_down)
    sigmoid_gate = jax.nn.sigmoid(gate_pre)
    hidden_act = (gate_pre * sigmoid_gate * up_pre).astype(jnp.bfloat16)
    gate_back = (
        grad_hidden * up_pre * sigmoid_gate * (1.0 + gate_pre * (1.0 - sigmoid_gate))
    ).astype(jnp.bfloat16)
    up_back = (grad_hidden * gate_pre * sigmoid_gate).astype(jnp.bfloat16)
    normed_terms = plain_dot(gate_back, g_gate) + plain_dot(up_back, g_up)
    pair_terms = jnp.concatenate([normed_terms, plain_dot(hidden_act, g_down)], 1)
    pair_sums = scatter_over(pair_terms.astype(jnp.bfloat16), PLANE, 2, kernels)
    normed_part, down_part = pair_sums[:, :width], pair_sums[:, width:]
    feed_terms = jnp.concatenate(
        [
            outer_dot(gate_back, normed_group),
            outer_dot(up_back, normed_group),
            outer_dot(hidden_act, cot_group),
        ],
        1,
    ).astype(jnp.bfloat16)
    feed_grads = scatter_sum(feed_terms, "z").astype(jnp.float32)
    layer_out = (middle + down_part).astype(jnp.bfloat16)
    grad_middle = cotangent.astype(jnp.float32) + norm_back(
        normed_part, middle, scale_ffn, gain_ffn
    )
    middle_bf = grad_middle.astype(jnp.bfloat16)
    grad_attended = proj_dot(middle_bf, w_out).astype(jnp.bfloat16)
    grad_attended = grad_attended.reshape(1, rows_here, KV_HEADS, repeat_count, HEAD_DIM)
    scores_again = attend_scores(query_bf, key_bf, allowed)
    soft = jnp.exp(scores_again - log_total)
    grad_soft = jnp.einsum(
        "grkpd,gskd->gkprs", grad_attended, value_bf, preferred_element_type=jnp.float32
    )
    grad_scores = (
        soft * (grad_soft - jnp.sum(soft * grad_soft, -1, keepdims=True)) * HEAD_DIM ** (-0.5)
    ).astype(jnp.bfloat16)
    grad_queries = jnp.einsum(
        "gkprs,gskd->grkpd", grad_scores, key_bf, preferred_element_type=jnp.float32
    )
    grad_queries = grad_queries.reshape(1, rows_here, HEADS, HEAD_DIM)
    grad_keys = jnp.einsum(
        "gkprs,grkpd->gskd", grad_scores, query_bf, preferred_element_type=jnp.float32
    )
    grad_values = jnp.einsum(
        "gkprs,grkpd->gskd",
        soft.astype(jnp.bfloat16),
        grad_attended,
        preferred_element_type=jnp.float32,
    )
    grad_queries = grad_queries * cosine + unrotate(grad_queries * sines)
    grad_keys = grad_keys * cosine + unrotate(grad_keys * sines)
    grad_projected = jnp.concatenate(
        [
            grad_queries.reshape(rows_here, q_width),
            grad_keys.reshape(rows_here, kv_width),
            grad_values.reshape(rows_here, kv_width),
        ],
        -1,
    )
    projected_bf = grad_projected.astype(jnp.bfloat16)
    grad_inputs = plain_dot(projected_bf, w_qkv)
    grad_tokens = (grad_middle + norm_back(grad_inputs, resid_in, scale_att, gain_att)).astype(
        jnp.bfloat16
    )
    attention_term = jnp.concatenate(
        [outer_dot(projected_bf, normed_att), outer_dot(attended, middle_bf)], 0
    )
    grad_attention = scatter_over(attention_term.astype(jnp.bfloat16), BOTH, 3, kernels)
    small_terms = jnp.concatenate(
        [
            jnp.sum(grad_inputs * resid_in * scale_att, 0),
            jnp.sum(normed_part * middle * scale_ffn, 0),
            jnp.sum(grad_projected, 0),
        ]
    )
    small_block = jnp.pad(small_terms, (0, -small_terms.size % 1024)).reshape(-1, 128)
    small_sums = jnp.sum(
        gather_over(small_block, BOTH, 4, kernels).reshape(-1, small_block.size), 0
    )
    return (
        layer_out,
        grad_tokens,
        small_sums[:width],
        small_sums[width : 2 * width],
        small_sums[2 * width : small_terms.size],
        grad_attention,
        feed_grads[:, :width],
        feed_grads[:, width : 2 * width],
        feed_grads[:, 2 * width :],
    )


def solution(mesh):
    dp, fsdp = mesh.shape["dp"], mesh.shape["fsdp"]
    kernels = (dp, fsdp) == (8, 4)
    finer = Mesh(mesh.devices.reshape(dp // 2, 2, fsdp // 2, 2), BOTH)
    placed = (
        P(BOTH, None),
        P(BOTH, None),
        P(BOTH, None),
        P(),
        P(),
        P(),
        P(BOTH, None),
        P(BOTH, None),
        P(BOTH, None),
        P(BOTH, None),
    )
    return jax.shard_map(
        functools.partial(on_device, kernels),
        mesh=finer,
        in_specs=placed,
        out_specs=(
            P(BOTH, None),
            P(BOTH, None),
            P(),
            P(),
            P(),
            P(BOTH, None),
            P(BOTH, None),
            P(BOTH, None),
            P(BOTH, None),
        ),
        check_vma=False,
    )
```

```python
import jax
import jax.numpy as jnp
import functools
from jax import lax
from jax.experimental import pallas as pl
from jax.experimental.pallas import tpu as pltpu
from jax.sharding import Mesh, PartitionSpec as P

HEADS = 14
KV_HEADS = 2
HEAD_DIM = 64
QKV = 1152


EPS = 1e-06
THETA = 1000000.0


def rotary_tables(segments):
    length = segments.shape[-1]
    before = jnp.sum((segments[..., None, :] < segments[..., :, None]).astype(jnp.int32), -1)
    positions = jnp.arange(length, dtype=jnp.int32)[None, :] - before
    halfway = HEAD_DIM // 2
    frequency = THETA ** (-2.0 * jnp.arange(halfway, dtype=jnp.float32) / HEAD_DIM)
    angles = positions.astype(jnp.float32)[..., None] * frequency
    cosine = jnp.concatenate([jnp.cos(angles), jnp.cos(angles)], -1)[:, :, None, :]
    sines = jnp.concatenate([jnp.sin(angles), jnp.sin(angles)], -1)[:, :, None, :]
    return (cosine, sines)


def rotate(tensor):
    halfway = tensor.shape[-1] // 2
    return jnp.concatenate([-tensor[..., halfway:], tensor[..., :halfway]], -1)


def unrotate(tensor):
    halfway = tensor.shape[-1] // 2
    return jnp.concatenate([tensor[..., halfway:], -tensor[..., :halfway]], -1)


def visible(segments):
    length = segments.shape[-1]
    matches = segments[..., :, None] == segments[..., None, :]
    index = jnp.arange(length, dtype=jnp.int32)
    causal = index[None, :] <= index[:, None]
    return matches & causal[None]


def attend_scores(query_bf, key_bf, allowed):
    scores = jnp.einsum(
        "grkpd,gskd->gkprs", query_bf, key_bf, preferred_element_type=jnp.float32
    ) * HEAD_DIM ** (-0.5)
    return jnp.where(allowed[:, None, None], scores, -1e30)


def norm_back(grad_in, values, scale, gain):
    weighted = grad_in * gain
    return scale * weighted - values * scale**3 * jnp.mean(weighted * values, -1, keepdims=True)


def plain_dot(left, right):
    return jnp.dot(left, right, preferred_element_type=jnp.float32)


def proj_dot(left, right):
    return lax.dot_general(
        left, right, (((1,), (1,)), ((), ())), preferred_element_type=jnp.float32
    )


def outer_dot(left, right):
    return lax.dot_general(
        left, right, (((0,), (0,)), ((), ())), preferred_element_type=jnp.float32
    )


PLANE = ("y", "x", "c")
BOTH = ("z",) + PLANE
OTHERS = ((1, 1), (0, 1), (1, 0))
MESH_ID = pl.DeviceIdType.MESH


def gather(shard, axes):
    return lax.all_gather(shard, axes, axis=0, tiled=True)


def scatter_sum(terms, axes):
    return lax.psum_scatter(terms, axes, scatter_dimension=0, tiled=True)


def here():
    return tuple(lax.axis_index(name) for name in BOTH)


def at_device(z, y, x, c):
    return {"z": z, "y": y, "x": x, "c": c}


def greet(count):
    z, y, x, c = here()
    barrier = pltpu.get_barrier_semaphore()
    targets = [at_device(lax.rem(z + k, count), y, x, c) for k in range(1, count)]
    targets += [at_device(z, y ^ dy, x ^ dx, c) for dy, dx in OTHERS]
    targets.append(at_device(z, y, x, 1 - c))
    for target in targets:
        pl.semaphore_signal(barrier, inc=1, device_id=target, device_id_type=MESH_ID)
    pl.semaphore_wait(barrier, len(targets))


def remote(source, target, send, recv, device):
    return pltpu.make_async_remote_copy(
        src_ref=source,
        dst_ref=target,
        send_sem=send,
        recv_sem=recv,
        device_id=device,
        device_id_type=MESH_ID,
    )


def gather_steps(count, shard, out, own_sem, z_send, z_recv, p_send, p_recv, c_send, c_recv):
    z, y, x, c = here()
    slot = z if count > 1 else 0
    own = pltpu.make_async_copy(shard, out.at[slot, y, x, c], own_sem)
    own.start()
    along_z = []
    for k in range(1, count):
        copy = remote(
            shard,
            out.at[slot, y, x, c],
            z_send.at[k - 1],
            z_recv.at[k - 1],
            at_device(lax.rem(z + k, count), y, x, c),
        )
        copy.start()
        along_z.append(copy)
    yield
    sent = []
    for k in range(count):
        if k:
            along_z[k - 1].wait_recv()
        held = lax.rem(z - k + count, count) if count > 1 else 0
        block = out.at[held, y, x, c]
        source = block if k else shard
        for j, (dy, dx) in enumerate(OTHERS):
            copy = remote(
                source, block, p_send.at[k, j], p_recv.at[k, j], at_device(z, y ^ dy, x ^ dx, c)
            )
            copy.start()
            sent.append((copy, k, j, held))
        copy = remote(source, block, c_send.at[k, 3], c_recv.at[k, 3], at_device(z, y, x, 1 - c))
        copy.start()
        along_z.append(copy)
    yield
    passed = []
    for copy, k, j, held in sent:
        dy, dx = OTHERS[j]
        copy.wait_recv()
        block = out.at[held, y ^ dy, x ^ dx, c]
        onward = remote(block, block, c_send.at[k, j], c_recv.at[k, j], at_device(z, y, x, 1 - c))
        onward.start()
        passed.append(onward)
    yield
    for copy, k, j, held in sent:
        copy.wait_send()
    for at, copy in enumerate(along_z):
        copy.wait_send()
        if at >= count - 1:
            copy.wait_recv()
    for copy in passed:
        copy.wait()
    own.wait()


def gather_kernel(count, *refs):
    greet(count)
    for _ in gather_steps(count, *refs):
        pass


def gather_sems(count):
    dma = pltpu.SemaphoreType.DMA
    pairs = ((3,), (3,), (count, 3), (count, 3), (count, 4), (count, 4))
    return [dma(())] + [dma(shape) for shape in pairs]


def kernel_gather(shard, count, ident):
    rows, width = shard.shape
    out = pl.pallas_call(
        functools.partial(gather_kernel, count),
        out_shape=jax.ShapeDtypeStruct((count, 2, 2, 2, rows, width), shard.dtype),
        in_specs=[pl.BlockSpec(memory_space=pltpu.VMEM)],
        out_specs=pl.BlockSpec(memory_space=pl.ANY),
        scratch_shapes=gather_sems(count),
        compiler_params=pltpu.CompilerParams(collective_id=ident, has_side_effects=True),
        cost_estimate=pl.CostEstimate(
            flops=20_000_000_000, bytes_accessed=8 * count * rows * width * 2, transcendentals=0
        ),
    )(shard)
    return out.reshape(count * 8 * rows, width)


def scatter_kernel(
    count, terms, small, out, small_out, c_buf, s_buf, p_buf, total, zs_buf, zr_buf,
    c_send, c_recv, p_send, p_recv, z_send, z_recv, *small_sems,
):
    z, y, x, c = here()
    greet(count)
    pieces = OTHERS + ((0, 0),)
    small_steps = gather_steps(count, small, small_out, *small_sems) if small_sems else iter(range(3))
    next(small_steps)
    across = []
    for j, (dy, dx) in enumerate(pieces):
        copy = remote(
            terms.at[:, y ^ dy, x ^ dx, 1 - c],
            c_buf.at[j],
            c_send.at[j],
            c_recv.at[j],
            at_device(z, y, x, 1 - c),
        )
        copy.start()
        across.append(copy)
    plane = []
    for j, (dy, dx) in enumerate(pieces):
        across[j].wait_recv()
        for k in range(count):
            pair = terms[k, y ^ dy, x ^ dx, c].astype(jnp.float32) + c_buf[j, k].astype(jnp.float32)
            if j < 3:
                s_buf[j, k] = pair.astype(jnp.bfloat16)
            else:
                total[k] = pair
        if j < 3:
            copy = remote(
                s_buf.at[j],
                p_buf.at[j],
                p_send.at[j],
                p_recv.at[j],
                at_device(z, y ^ dy, x ^ dx, c),
            )
            copy.start()
            plane.append(copy)
        if j == 0:
            next(small_steps)
    next(small_steps)
    for copy in plane:
        copy.wait_recv()
    if count == 1:
        out[...] = (
            total[0]
            + p_buf[0, 0].astype(jnp.float32)
            + p_buf[1, 0].astype(jnp.float32)
            + p_buf[2, 0].astype(jnp.float32)
        )
    along = []
    for k in range(1, count):
        other = lax.rem(z + k, count)
        zs_buf[k - 1] = (
            total[other]
            + p_buf[0, other].astype(jnp.float32)
            + p_buf[1, other].astype(jnp.float32)
            + p_buf[2, other].astype(jnp.float32)
        ).astype(jnp.bfloat16)
        copy = remote(
            zs_buf.at[k - 1],
            zr_buf.at[k - 1],
            z_send.at[k - 1],
            z_recv.at[k - 1],
            at_device(other, y, x, c),
        )
        copy.start()
        along.append(copy)
    if count > 1:
        kept = (
            total[z]
            + p_buf[0, z].astype(jnp.float32)
            + p_buf[1, z].astype(jnp.float32)
            + p_buf[2, z].astype(jnp.float32)
        )
        for k in range(1, count):
            along[k - 1].wait_recv()
            kept = kept + zr_buf[k - 1].astype(jnp.float32)
        out[...] = kept
    for copy in across + plane + along:
        copy.wait_send()
    for _ in small_steps:
        pass


def plane_kernel(terms, out, *rest):
    scatter_kernel(1, terms, None, out, None, *rest)


def kernel_scatter(terms, small, count, ident):
    rows, width = terms.shape[0] // (8 * count), terms.shape[1]
    dma = pltpu.SemaphoreType.DMA
    block = (rows, width)
    extra = block if count > 1 else (16, 128)
    vmem = pl.BlockSpec(memory_space=pltpu.VMEM)
    sums = jax.ShapeDtypeStruct(block, jnp.float32)
    if small is not None:
        parts = jax.ShapeDtypeStruct((count, 2, 2, 2) + small.shape, small.dtype)
    return pl.pallas_call(
        plane_kernel if small is None else functools.partial(scatter_kernel, count),
        out_shape=sums if small is None else (sums, parts),
        in_specs=[vmem] if small is None else [vmem, vmem],
        out_specs=vmem if small is None else (vmem, pl.BlockSpec(memory_space=pl.ANY)),
        scratch_shapes=[
            pltpu.VMEM((4, count) + block, jnp.bfloat16),
            pltpu.VMEM((3, count) + block, jnp.bfloat16),
            pltpu.VMEM((3, count) + block, jnp.bfloat16),
            pltpu.VMEM((count,) + block, jnp.float32),
            pltpu.VMEM((3,) + extra, jnp.bfloat16),
            pltpu.VMEM((3,) + extra, jnp.bfloat16),
            dma((4,)),
            dma((4,)),
            dma((3,)),
            dma((3,)),
            dma((3,)),
            dma((3,)),
        ]
        + ([] if small is None else gather_sems(count)),
        compiler_params=pltpu.CompilerParams(collective_id=ident, has_side_effects=True),
        cost_estimate=pl.CostEstimate(
            flops=20_000_000_000, bytes_accessed=8 * count * rows * width * 2, transcendentals=0
        ),
    )(terms.reshape((count, 2, 2, 2) + block), *([] if small is None else [small]))


def gather_over(shard, axes, ident, kernels):
    if not kernels:
        return gather(shard, axes)
    return kernel_gather(shard, lax.axis_size("z") if axes == BOTH else 1, ident)


def plane_sums(terms, kernels):
    if not kernels:
        return scatter_sum(terms, PLANE).astype(jnp.float32)
    return kernel_scatter(terms, None, 1, 2)


def scatter_over(terms, small, axes, ident, kernels):
    if not kernels:
        parts = lax.all_gather(small, axes, axis=0, tiled=False)
        sums = scatter_sum(terms, axes).astype(jnp.float32)
    else:
        sums, parts = kernel_scatter(
            terms, small, lax.axis_size("z") if axes == BOTH else 1, ident
        )
    return sums, jnp.sum(parts.reshape(-1, small.size), 0)


def on_device(
    kernels, tokens, cotangent, segments, gain_att, gain_ffn, qkv_bias, w_attention, w_gate, w_up, w_down
):
    w_all = gather_over(w_attention, BOTH, 0, kernels)
    w_qkv, w_out = w_all[:QKV], w_all[QKV:]
    width = tokens.shape[1]
    w_feed = gather(jnp.concatenate([w_gate, w_up, w_down], 1), "z")
    g_gate, g_up, g_down = w_feed[:, :width], w_feed[:, width : 2 * width], w_feed[:, 2 * width :]
    rows_here = tokens.shape[0]
    q_width = HEADS * HEAD_DIM
    kv_width = KV_HEADS * HEAD_DIM
    repeat_count = HEADS // KV_HEADS
    resid_in = tokens.astype(jnp.float32)
    scale_att = lax.rsqrt(jnp.mean(resid_in * resid_in, -1, keepdims=True) + EPS)
    normed_att = (resid_in * scale_att * gain_att).astype(jnp.bfloat16)
    projected = proj_dot(normed_att, w_qkv) + qkv_bias
    cosine, sines = rotary_tables(segments)
    queries = projected[:, :q_width].reshape(1, rows_here, HEADS, HEAD_DIM)
    keys_raw = projected[:, q_width : q_width + kv_width].reshape(1, rows_here, KV_HEADS, HEAD_DIM)
    values_raw = projected[:, q_width + kv_width :].reshape(1, rows_here, KV_HEADS, HEAD_DIM)
    query_bf = (
        (queries * cosine + rotate(queries) * sines)
        .astype(jnp.bfloat16)
        .reshape(1, rows_here, KV_HEADS, repeat_count, HEAD_DIM)
    )
    key_bf = (keys_raw * cosine + rotate(keys_raw) * sines).astype(jnp.bfloat16)
    value_bf = values_raw.astype(jnp.bfloat16)
    allowed = visible(segments)
    scores = attend_scores(query_bf, key_bf, allowed)
    log_total = jnp.log(jnp.sum(jnp.exp(scores), -1, keepdims=True))
    soft_bf = jnp.exp(scores - log_total).astype(jnp.bfloat16)
    attended = jnp.einsum(
        "gkprs,gskd->grkpd", soft_bf, value_bf, preferred_element_type=jnp.float32
    )
    attended = attended.reshape(rows_here, q_width).astype(jnp.bfloat16)
    middle = resid_in + plain_dot(attended, w_out)
    scale_ffn = lax.rsqrt(jnp.mean(middle * middle, -1, keepdims=True) + EPS)
    normed_ffn = (middle * scale_ffn * gain_ffn).astype(jnp.bfloat16)
    pair_group = gather_over(jnp.concatenate([normed_ffn, cotangent], 1), PLANE, 1, kernels)
    normed_group, cot_group = pair_group[:, :width], pair_group[:, width:]
    gate_pre = proj_dot(normed_group, g_gate)
    up_pre = proj_dot(normed_group, g_up)
    grad_hidden = proj_dot(cot_group, g_down)
    sigmoid_gate = jax.nn.sigmoid(gate_pre)
    hidden_act = (gate_pre * sigmoid_gate * up_pre).astype(jnp.bfloat16)
    gate_back = (
        grad_hidden * up_pre * sigmoid_gate * (1.0 + gate_pre * (1.0 - sigmoid_gate))
    ).astype(jnp.bfloat16)
    up_back = (grad_hidden * gate_pre * sigmoid_gate).astype(jnp.bfloat16)
    normed_terms = plain_dot(gate_back, g_gate) + plain_dot(up_back, g_up)
    pair_terms = jnp.concatenate([normed_terms, plain_dot(hidden_act, g_down)], 1)
    feed_terms = jnp.concatenate(
        [
            outer_dot(gate_back, normed_group),
            outer_dot(up_back, normed_group),
            outer_dot(hidden_act, cot_group),
        ],
        1,
    ).astype(jnp.bfloat16)
    pair_terms, feed_terms = lax.optimization_barrier(
        (pair_terms.astype(jnp.bfloat16), feed_terms)
    )
    feed_grads = scatter_sum(feed_terms, "z").astype(jnp.float32)
    pair_sums = plane_sums(pair_terms, kernels)
    normed_part, down_part = pair_sums[:, :width], pair_sums[:, width:]
    layer_out = (middle + down_part).astype(jnp.bfloat16)
    grad_middle = cotangent.astype(jnp.float32) + norm_back(
        normed_part, middle, scale_ffn, gain_ffn
    )
    middle_bf = grad_middle.astype(jnp.bfloat16)
    grad_attended = proj_dot(middle_bf, w_out).astype(jnp.bfloat16)
    grad_attended = grad_attended.reshape(1, rows_here, KV_HEADS, repeat_count, HEAD_DIM)
    scores_again = attend_scores(query_bf, key_bf, allowed)
    soft = jnp.exp(scores_again - log_total)
    grad_soft = jnp.einsum(
        "grkpd,gskd->gkprs", grad_attended, value_bf, preferred_element_type=jnp.float32
    )
    grad_scores = (
        soft * (grad_soft - jnp.sum(soft * grad_soft, -1, keepdims=True)) * HEAD_DIM ** (-0.5)
    ).astype(jnp.bfloat16)
    grad_queries = jnp.einsum(
        "gkprs,gskd->grkpd", grad_scores, key_bf, preferred_element_type=jnp.float32
    )
    grad_queries = grad_queries.reshape(1, rows_here, HEADS, HEAD_DIM)
    grad_keys = jnp.einsum(
        "gkprs,grkpd->gskd", grad_scores, query_bf, preferred_element_type=jnp.float32
    )
    grad_values = jnp.einsum(
        "gkprs,grkpd->gskd",
        soft.astype(jnp.bfloat16),
        grad_attended,
        preferred_element_type=jnp.float32,
    )
    grad_queries = grad_queries * cosine + unrotate(grad_queries * sines)
    grad_keys = grad_keys * cosine + unrotate(grad_keys * sines)
    grad_projected = jnp.concatenate(
        [
            grad_queries.reshape(rows_here, q_width),
            grad_keys.reshape(rows_here, kv_width),
            grad_values.reshape(rows_here, kv_width),
        ],
        -1,
    )
    projected_bf = grad_projected.astype(jnp.bfloat16)
    grad_inputs = plain_dot(projected_bf, w_qkv)
    grad_tokens = (grad_middle + norm_back(grad_inputs, resid_in, scale_att, gain_att)).astype(
        jnp.bfloat16
    )
    attention_term = jnp.concatenate(
        [outer_dot(projected_bf, normed_att), outer_dot(attended, middle_bf)], 0
    )
    small_terms = jnp.concatenate(
        [
            jnp.sum(grad_inputs * resid_in * scale_att, 0),
            jnp.sum(normed_part * middle * scale_ffn, 0),
            jnp.sum(grad_projected, 0),
        ]
    )
    small_block = jnp.pad(small_terms, (0, -small_terms.size % 1024)).reshape(-1, 128)
    grad_attention, small_sums = scatter_over(
        attention_term.astype(jnp.bfloat16), small_block, BOTH, 3, kernels
    )
    return (
        layer_out,
        grad_tokens,
        small_sums[:width],
        small_sums[width : 2 * width],
        small_sums[2 * width : small_terms.size],
        grad_attention,
        feed_grads[:, :width],
        feed_grads[:, width : 2 * width],
        feed_grads[:, 2 * width :],
    )


def solution(mesh):
    dp, fsdp = mesh.shape["dp"], mesh.shape["fsdp"]
    kernels = (dp, fsdp) == (8, 4)
    finer = Mesh(mesh.devices.reshape(dp // 2, 2, fsdp // 2, 2), BOTH)
    placed = (
        P(BOTH, None),
        P(BOTH, None),
        P(BOTH, None),
        P(),
        P(),
        P(),
        P(BOTH, None),
        P(BOTH, None),
        P(BOTH, None),
        P(BOTH, None),
    )
    return jax.shard_map(
        functools.partial(on_device, kernels),
        mesh=finer,
        in_specs=placed,
        out_specs=(
            P(BOTH, None),
            P(BOTH, None),
            P(),
            P(),
            P(),
            P(BOTH, None),
            P(BOTH, None),
            P(BOTH, None),
            P(BOTH, None),
        ),
        check_vma=False,
    )
```
